768 devices in a mesh: dp: 16 (over y, core), section: 48 (over x, z).
Axes of the slice: x: 4, y: 8, z: 12, core: 2. Of those that a mesh axis runs over, the one named last changes fastest.
Arguments:
- lat_raw: bfloat16 [48, 16, 16, 16], P('section', None, 'dp'), may hold values from -6 to 6
- txt_raw: bfloat16 [48, 16, 16, 4096], P('section', None, 'dp'), may hold values from -6 to 6
- lat_embed: bfloat16 [16, 1024], replicated, may hold values from -1.5 to 1.5
- txt_embed: bfloat16 [4096, 1024], replicated, may hold values from -0.09375 to 0.09375
- image_owner: int32 [48, 16], replicated, may hold values from 0 to 15, each once within a row
- text_len: int32 [48, 16], replicated, may hold values from 1 to 16
- weights: bfloat16 [48, 1024, 1024], P('section', 'dp'), may hold values from -0.1875 to 0.1875
- top_grad: bfloat16 [16, 48, 32, 1024], P('dp', 'section'), may hold values from -0.75 to 0.75
Outputs:
- weight_grads: float32 [48, 1024, 1024], P('section', 'dp')
The draws below stay inside these ranges and needn't reach their ends.
Inputs may be any that keep to these rules, and one draw needn't show every extreme that they name: `image_owner`: each row names every data shard exactly once.
All inputs are finite; a program needn't handle non-finite values.
Results may differ from the reference program's by a relative error of at most 0.023.
Values may be sent and summed in bfloat16 or wider, within the bound.
A program may use at most 32 MiB of HBM per device.

```python
import jax
import jax.numpy as jnp
from jax import lax

C = 1024
TXT_IN = 4096
LAT_IN = 16
LAT = 16
TXT = 16
PIPE = 8
ROWS = 32
N_DP = 16
N_SECTION = 48


def with_ends(values, stream_key, smallest, top_value):
    place = [jax.random.randint(jax.random.fold_in(stream_key, axis), (), 0, length) for axis, length in enumerate(values.shape)]
    longest = values.shape.index(max(values.shape))
    next_to = place[:longest] + [(place[longest] + 1) % values.shape[longest]] + place[longest + 1:]
    return values.at[tuple(place)].set(smallest).at[tuple(next_to)].set(top_value)


def steps_of(rng, extent, split, low, top_value):
    factor_of, own = 1.0, jax.random.fold_in(rng, 6)
    for dim, parts in split:
        draws = jnp.exp(jax.random.uniform(jax.random.fold_in(own, dim), (parts,), jnp.float32, low / len(split), top_value / len(split)))
        factor_of = factor_of * jnp.repeat(draws, extent[dim] // parts).reshape([-1 if axis == dim else 1 for axis in range(len(extent))])
    return factor_of


def scatter_about(rng, shape, spread, bound, split=(), dtype=jnp.bfloat16):
    loudness = steps_of(rng, shape, split, -0.22, 0.18) if split else 1.0
    array = jax.random.normal(rng, shape, jnp.float32) * spread * loudness
    return jnp.minimum(jnp.maximum(array, -bound), bound).astype(dtype)


def setup_inputs(seed: int = 0) -> dict:
    key_of = jax.random.split(jax.random.key(seed), 9)
    lat_raw = scatter_about(key_of[0], (N_SECTION, N_DP, LAT, LAT_IN), 1.0, 6.0, ((0, 48), (2, 16)))
    txt_raw = scatter_about(key_of[1], (N_SECTION, N_DP, TXT, TXT_IN), 1.0, 6.0, ((0, 48), (2, 16)))
    lat_embed = scatter_about(key_of[2], (LAT_IN, C), LAT_IN ** -0.5, 1.5)
    txt_embed = scatter_about(key_of[3], (TXT_IN, C), TXT_IN ** -0.5, 0.09375)
    image_owner = jax.vmap(lambda own: jax.random.permutation(own, N_DP))(jax.random.split(key_of[4], N_SECTION)).reshape((N_SECTION, N_DP)).astype(jnp.int32)
    text_len = with_ends(jax.random.randint(key_of[5], (N_SECTION, N_DP), 1, TXT + 1), jax.random.fold_in(key_of[5], 1), 1, TXT).astype(jnp.int32)
    weights = scatter_about(key_of[6], (N_SECTION, C, C), C ** -0.5, 0.1875, ((0, 48), (1, 16)))
    top_grad = scatter_about(key_of[7], (N_DP, N_SECTION, ROWS, C), 0.05, 0.75, ((0, 16), (1, 48)))
    return dict(lat_raw=lat_raw, txt_raw=txt_raw, lat_embed=lat_embed, txt_embed=txt_embed, image_owner=image_owner, text_len=text_len, weights=weights, top_grad=top_grad)


norm_eps = 1e-06

def modulate(tokens_in, text_mask, text_count):
    inv_norm = lax.rsqrt(lax.optimization_barrier(jnp.mean(tokens_in * tokens_in, axis=1, keepdims=True)) + norm_eps)
    normed = tokens_in * inv_norm
    pooled = 0.5 * lax.optimization_barrier(jnp.sum(normed * text_mask[:, None], axis=0)) / text_count
    return normed * (1.0 + pooled)[None, :]

def silu_slope(gate_preactivation):
    sigmoid_v = jax.nn.sigmoid(gate_preactivation)
    return sigmoid_v * (1.0 + gate_preactivation * (1.0 - sigmoid_v))

def reference(lat_raw, txt_raw, lat_embed, txt_embed, image_owner, text_len, weights, top_grad):
    lat_enc = jnp.einsum('sjrc,cf->sjrf', lat_raw.astype(jnp.float32), lat_embed.astype(jnp.float32)).astype(jnp.bfloat16)
    text_enc = jnp.einsum('sjrc,cf->sjrf', txt_raw.astype(jnp.float32), txt_embed.astype(jnp.float32)).astype(jnp.bfloat16)
    images = jnp.concatenate([lat_enc, text_enc], axis=2)
    senders = jnp.argsort(image_owner, axis=1, stable=True).astype(jnp.int32)
    positions = jnp.arange(LAT + TXT).astype(jnp.int32)
    batch_mod = jax.vmap(modulate)
    micro_range = jnp.arange(PIPE).astype(jnp.int32)
    results = []
    for group_idx in range(N_SECTION // PIPE):
        first_col = group_idx * PIPE
        lane_images = images[first_col:first_col + PIPE]
        lane_send = senders[first_col:first_col + PIPE]
        lane_len = text_len[first_col:first_col + PIPE].astype(jnp.int32)
        portion_weight = weights[first_col:first_col + PIPE].astype(jnp.float32)
        lane_tops = top_grad[:, first_col:first_col + PIPE]

        def one_lane(total_grad, my_shard):
            src_slots = lane_send[:, my_shard]
            current = lane_images[micro_range, src_slots]
            lengths = lane_len[micro_range, src_slots]
            text_masks = ((positions[None, :] >= LAT) & (positions[None, :] < LAT + lengths[:, None])).astype(jnp.float32)
            counts = lengths.astype(jnp.float32)
            top_rows = lax.dynamic_index_in_dim(lane_tops, my_shard, 0, keepdims=False)[::-1]
            inputs = []
            for portion_index in range(PIPE):
                inputs.append(current)
                widened = current.astype(jnp.float32)
                hidden_layer_state = batch_mod(widened, text_masks, counts).astype(jnp.bfloat16)
                gate_preactivation = jnp.einsum('xat,tg->xag', hidden_layer_state.astype(jnp.float32), portion_weight[portion_index])
                current = (widened + jax.nn.silu(gate_preactivation)).astype(jnp.bfloat16)
            grad_rows = top_rows
            portion_gradient = []
            for portion_index in reversed(range(PIPE)):
                widened = inputs[portion_index].astype(jnp.float32)
                hidden_wide, pullback = jax.vjp(lambda values: batch_mod(values, text_masks, counts), widened)
                hidden_layer_state = hidden_wide.astype(jnp.bfloat16)
                gate_preactivation = jnp.einsum('xat,tg->xag', hidden_layer_state.astype(jnp.float32), portion_weight[portion_index])
                derivative_rows = (grad_rows.astype(jnp.float32) * silu_slope(gate_preactivation)).astype(jnp.bfloat16)
                portion_gradient.append(jnp.einsum('xza,xzi->ai', hidden_layer_state.astype(jnp.float32), derivative_rows.astype(jnp.float32)))
                reverse_sweep = jnp.einsum('adp,lp->adl', derivative_rows.astype(jnp.float32), portion_weight[portion_index])
                grad_rows = (grad_rows.astype(jnp.float32) + pullback(reverse_sweep)[0]).astype(jnp.bfloat16)
            return (total_grad + jnp.stack(portion_gradient[::-1]), None)
        total_grad, _ = lax.scan(one_lane, jnp.zeros((PIPE, C, C), jnp.float32), jnp.arange(N_DP).astype(jnp.int32))
        results.append(total_grad)
    return jnp.concatenate(results, axis=0)
```

```python
import functools

import jax
import jax.numpy as jnp
from jax import lax
from jax.experimental import pallas as pl
from jax.experimental.pallas import tpu as pltpu
from jax.sharding import PartitionSpec as P

NORM_EPS = 1e-06
MESH = pl.DeviceIdType.MESH
F32 = jnp.float32
BF16 = jnp.bfloat16
EMB_CHUNKS = 4
FWD_CHUNKS = 2


def step_kernel(
    n_dp,
    pipe,
    owner_ref,
    len_ref,
    lat_ref,
    txt_ref,
    lat_emb_ref,
    emb_hbm,
    w_ref,
    top_ref,
    out_ref,
    emb,
    wfull,
    route_out,
    route_in,
    rows_f32,
    x0,
    coef,
    xin,
    xout,
    gin,
    gout,
    gate_slope,
    hid_send,
    hid,
    slopes,
    partial,
    rs_out,
    rs_in,
    emb_sem,
    route_sem,
    w_send,
    w_recv,
    pw_send,
    pw_recv,
    feed_sem,
    x_send,
    x_recv,
    g_send,
    g_recv,
    h_sem,
    s_sem,
    r_send,
    r_recv,
):
    chips = n_dp // 2
    half_ring = chips // 2
    channels = wfull.shape[0]
    share = channels // n_dp
    half = share // 2
    rows = 2 * n_dp
    me = lax.axis_index("dp")
    section = lax.axis_index("section")
    pos = lax.rem(section, pipe)
    first = section - pos
    last = first + pipe - 1
    chip = lax.div(me, 2)
    core = lax.rem(me, 2)
    partner = chip * 2 + 1 - core
    beside = first + lax.rem(pos + 1, max(pipe, 1))

    def remote(src, dst, send, recv, **where):
        return pltpu.make_async_remote_copy(
            src_ref=src,
            dst_ref=dst,
            send_sem=send,
            recv_sem=recv,
            device_id=where,
            device_id_type=MESH,
        )

    depth = emb.shape[0] // EMB_CHUNKS

    def emb_copy(i):
        part = pl.ds(i * depth, depth)
        return pltpu.make_async_copy(emb_hbm.at[part], emb.at[part], emb_sem.at[i])

    for i in range(EMB_CHUNKS):
        emb_copy(i).start()

    barrier = pltpu.get_barrier_semaphore()
    for k in range(1, n_dp):
        pl.semaphore_signal(
            barrier, inc=1, device_id={"dp": lax.rem(me + k, n_dp)}, device_id_type=MESH
        )
    for k in range(1, pipe):
        pl.semaphore_signal(
            barrier,
            inc=1,
            device_id={"section": first + lax.rem(pos + k, pipe)},
            device_id_type=MESH,
        )

    block = pl.ds(pl.multiple_of(first, pipe), pipe)
    mine = owner_ref[block, :] == me
    counts = jnp.sum(
        jnp.where(mine, len_ref[block, :], 0).astype(F32), axis=1, keepdims=True
    )
    order = lax.broadcasted_iota(jnp.int32, (n_dp, 128), 0).astype(F32)
    for m in range(pipe):
        count = jnp.broadcast_to(counts[m : m + 1, :], (n_dp, 128))
        coef[m] = jnp.where(order < count, 0.5 / count, 0.0)
    spot = lax.broadcasted_iota(jnp.int32, (n_dp, n_dp), 0)
    pick = (spot == owner_ref[pl.ds(section, 1), :]).astype(F32).astype(BF16)

    wfull[pl.ds(pl.multiple_of(me * share, share), share), :] = w_ref[...]
    pl.semaphore_wait(barrier, n_dp - 1 + pipe - 1)

    def w_block(owner_chip, whose, h):
        start = (owner_chip * 2 + whose) * share + h * half
        return wfull.at[pl.ds(pl.multiple_of(start, half), half)]

    def origin(direction, t):
        step = t if direction == 0 else chips - t
        return lax.rem(chip - step + 2 * chips, chips) if direction == 0 else lax.rem(chip + t, chips)

    def ahead(direction):
        step = 1 if direction == 0 else chips - 1
        return lax.rem(chip + step, chips) * 2 + core

    def halves(direction, t):
        if t == half_ring:
            return (direction,)
        return (0, 1)

    def w_hop(direction, t, h):
        src = w_ref.at[pl.ds(h * half, half)] if t == 1 else w_block(origin(direction, t - 1), core, h)
        dst = w_block(origin(direction, t - 1) if t > 1 else chip, core, h)
        return remote(
            src, dst, w_send.at[direction, t - 1, h], w_recv.at[direction, t - 1, h], dp=ahead(direction)
        )

    def w_land(direction, t, h):
        dst = w_block(origin(direction, t), core, h)
        return remote(
            dst, dst, w_send.at[direction, t - 1, h], w_recv.at[direction, t - 1, h], dp=ahead(direction)
        )

    def w_share(direction, t, h):
        blk = w_block(origin(direction, t), core, h)
        return remote(blk, blk, pw_send.at[direction, t, h], pw_recv.at[direction, t, h], dp=partner)

    def w_shared(direction, t, h):
        blk = w_block(origin(direction, t), 1 - core, h)
        return remote(blk, blk, pw_send.at[direction, t, h], pw_recv.at[direction, t, h], dp=partner)

    def w_own():
        blk = wfull.at[pl.ds(pl.multiple_of(me * share, share), share)]
        return remote(w_ref, blk, pw_send.at[0, 0, 0], pw_recv.at[0, 0, 0], dp=partner)

    def w_owned():
        blk = wfull.at[pl.ds(pl.multiple_of(partner * share, share), share)]
        return remote(w_ref, blk, pw_send.at[0, 0, 0], pw_recv.at[0, 0, 0], dp=partner)

    if half_ring:
        for h in (0, 1):
            for direction in (0, 1):
                if h in halves(direction, 1):
                    w_hop(direction, 1, h).start()
    w_own().start()

    def top_feed(slot):
        return remote(top_ref, gin.at[slot], feed_sem.at[0], g_recv.at[slot], section=last)

    @pl.when(pos < pipe - 1)
    def _():
        top_feed(pipe - 1 - pos).start()

    @pl.when(pos == pipe - 1)
    def _():
        gin[0] = top_ref[...]

    def encode(i, so_far):
        emb_copy(i).wait()
        part = pl.ds(i * depth, depth)
        return so_far + jnp.dot(txt_ref[:, part], emb[part, :], preferred_element_type=F32)

    def ring_step(t):
        for h in (0, 1):
            for direction in (0, 1):
                if h in halves(direction, t):
                    w_land(direction, t, h).wait_recv()
                    if t < half_ring and h in halves(direction, t + 1):
                        w_hop(direction, t + 1, h).start()
                    w_share(direction, t, h).start()

    text = jnp.zeros((n_dp, channels), F32)
    for i in range(EMB_CHUNKS):
        text = encode(i, text)
    lat = jnp.dot(lat_ref[...], lat_emb_ref[...], preferred_element_type=F32)
    lat_sel = jnp.dot(pick, lat.astype(BF16), preferred_element_type=F32)
    text_sel = jnp.dot(pick, text.astype(BF16), preferred_element_type=F32)
    for i in range(n_dp):
        route_out[i, 0:1, :] = lat_sel[i : i + 1, :]
        route_out[i, 1:2, :] = text_sel[i : i + 1, :]

    def route(k):
        to = lax.rem(me + k, n_dp)
        return remote(route_out.at[to], route_in.at[me], route_sem.at[0], route_sem.at[1], dp=to)

    for k in range(1, n_dp):
        route(k).start()
    route_in[me] = route_out[me]
    if half_ring:
        ring_step(1)

    several = pl.ds(0, n_dp - 1)
    routed = remote(
        route_out.at[several], route_in.at[several], route_sem.at[0], route_sem.at[1], dp=partner
    )
    routed.wait_recv()
    for i in range(n_dp):
        rows_f32[i : i + 1, :] = route_in[i, 0:1, :]
        rows_f32[n_dp + i : n_dp + i + 1, :] = route_in[i, 1:2, :]
    x0[...] = rows_f32[...].astype(BF16)

    def row_feed(slot):
        return remote(x0, xin.at[slot], feed_sem.at[1], x_recv.at[slot], section=first)

    @pl.when(pos > 0)
    def _():
        row_feed(pos).start()

    @pl.when(pos == 0)
    def _():
        xin[0] = rows_f32[...].astype(BF16)

    for t in range(2, half_ring + 1):
        ring_step(t)
    w_owned().wait_recv()
    for t in range(1, half_ring + 1):
        for h in (0, 1):
            for direction in (0, 1):
                if h in halves(direction, t):
                    w_shared(direction, t, h).wait_recv()

    text_rows = slice(n_dp, rows)
    low = lax.broadcasted_iota(jnp.int32, (rows, 128), 1) < 64
    spread = channels // 128

    def wide(column):
        return jnp.concatenate([column] * spread, axis=1)

    def normed(m):
        x = xin[m].astype(F32)
        inv = lax.rsqrt(jnp.mean(x * x, axis=1, keepdims=True) + NORM_EPS)
        u = x * inv
        pooled = jnp.sum(u[text_rows, :] * wide(coef[m]), axis=0, keepdims=True)
        return x, inv, u, 1.0 + pooled

    cols = channels // FWD_CHUNKS

    def x_hop(m, n):
        part = pl.ds(n * cols, cols)
        return remote(
            xout.at[m, :, part], xin.at[m, :, part], x_send, x_recv.at[m], section=section + 1
        )

    def hid_hop(m):
        return remote(hid_send.at[m], hid.at[1, m], h_sem.at[0], h_sem.at[1], dp=partner)

    def slope_hop(m):
        return remote(slopes.at[0, m], slopes.at[1, m], s_sem.at[0], s_sem.at[1], dp=partner)

    def forward(m, carry):
        @pl.when((pos > 0) | (m > 0))
        def _():
            remote(xout.at[m], xin.at[m], x_send, x_recv.at[m], section=beside).wait_recv()

        x, inv, u, scale = normed(m)
        hidden_wide = u * scale
        hidden = hidden_wide.astype(BF16)
        for n in range(FWD_CHUNKS):
            part = slice(n * cols, (n + 1) * cols)
            pre = jnp.dot(hidden, wfull[:, part], preferred_element_type=F32)
            sig = jax.nn.sigmoid(pre)
            xout[m, :, part] = (x[:, part] + pre * sig).astype(BF16)

            @pl.when(pos < pipe - 1)
            def _():
                x_hop(m, n).start()

            gate_slope[m, :, part] = sig * (1.0 + pre * (1.0 - sig))
        for k in range(chips // 2):
            a = hidden_wide[:, 256 * k : 256 * k + 128]
            b = hidden_wide[:, 256 * k + 128 : 256 * k + 256]
            lo = jnp.where(low, a, pltpu.roll(b, 64, 1))
            hi = jnp.where(low, pltpu.roll(a, 64, 1), b)
            place = slice(128 * k, 128 * k + 128)
            is_low = core == 0
            hid[0, m, :, place] = jnp.where(is_low, lo, hi).astype(BF16)
            hid_send[m, :, place] = jnp.where(is_low, hi, lo).astype(BF16)
        hid_hop(m).start()
        return carry

    lax.fori_loop(0, pipe, forward, 0)

    def g_hop(m):
        return remote(gout.at[m], gin.at[m], g_send, g_recv.at[m], section=section - 1)

    def backward(m, carry):
        x, inv, u, scale = normed(m)

        @pl.when((pos < pipe - 1) | (m > 0))
        def _():
            remote(gout.at[m], gin.at[m], g_send, g_recv.at[m], section=beside).wait_recv()

        g = gin[m].astype(F32)
        slope = (g * gate_slope[m]).astype(BF16)
        slopes[0, m] = slope
        back = lax.dot_general(
            slope, wfull[...], (((1,), (1,)), ((), ())), preferred_element_type=F32
        )
        to_pool = jnp.sum(back * u, axis=0, keepdims=True)
        gu = back * scale
        gu = jnp.concatenate(
            [gu[:n_dp, :], gu[text_rows, :] + wide(coef[m]) * to_pool], axis=0
        )
        along = jnp.mean(gu * u, axis=1, keepdims=True)
        gout[m] = (g + inv * (gu - u * along)).astype(BF16)

        @pl.when(pos > 0)
        def _():
            g_hop(m).start()

        slope_hop(m).start()
        return carry

    lax.fori_loop(0, pipe, backward, 0)

    def all_hid():
        return remote(hid_send, hid.at[1], h_sem.at[0], h_sem.at[1], dp=partner)

    def all_slopes():
        return remote(slopes.at[0], slopes.at[1], s_sem.at[0], s_sem.at[1], dp=partner)

    all_hid().wait_recv()
    all_slopes().wait_recv()
    deep = 2 * pipe * rows
    cotangents = slopes[...].reshape(deep, channels)
    for k in range(chips // 2):
        held = hid[:, :, :, 128 * k : 128 * k + 128].reshape(deep, 128)
        both = lax.dot_general(
            held, cotangents, (((0,), (0,)), ((), ())), preferred_element_type=F32
        )
        for j in (0, 1):
            for h in (0, 1):
                at = 64 * j + half * h
                partial[2 * k + j, h] = both[at : at + half, :]

    def r_hop(direction, t, h):
        return remote(
            rs_out.at[direction, t - 1, h],
            rs_in.at[direction, t - 1, h],
            r_send.at[direction, t - 1, h],
            r_recv.at[direction, t - 1, h],
            dp=ahead(direction),
        )

    def r_halves(direction, t):
        return (direction,) if t == 1 else (0, 1)

    for t in range(1, half_ring + 1):
        gap = half_ring - t + 1
        for h in (0, 1):
            for direction in (0, 1):
                if h in r_halves(direction, t):
                    to = lax.rem(chip + (gap if direction == 0 else chips - gap), chips)
                    total = partial[to, h]
                    if t > 1 and h in r_halves(direction, t - 1):
                        r_hop(direction, t - 1, h).wait_recv()
                        total = total + rs_in[direction, t - 2, h].astype(F32)
                    rs_out[direction, t - 1, h] = total.astype(BF16)
                    r_hop(direction, t, h).start()
    for h in (0, 1):
        total = partial[chip, h]
        for direction in (0, 1):
            if half_ring and h in r_halves(direction, half_ring):
                r_hop(direction, half_ring, h).wait_recv()
                total = total + rs_in[direction, half_ring - 1, h].astype(F32)
        out_ref[h * half : (h + 1) * half, :] = total

    for t in range(1, half_ring + 1):
        for h in (0, 1):
            for direction in (0, 1):
                if h in halves(direction, t):
                    w_hop(direction, t, h).wait_send()
                    w_share(direction, t, h).wait_send()
                if h in r_halves(direction, t):
                    r_hop(direction, t, h).wait_send()
    w_own().wait_send()
    routed.wait_send()
    all_hid().wait_send()
    all_slopes().wait_send()

    @pl.when(pos < pipe - 1)
    def _():
        top_feed(0).wait_send()
        remote(xout, xin, x_send, x_recv.at[0], section=beside).wait_send()

    @pl.when(pos > 0)
    def _():
        row_feed(0).wait_send()
        remote(gout, gin, g_send, g_recv.at[0], section=beside).wait_send()


def local(pipe, n_dp, lat_raw, txt_raw, lat_embed, txt_embed, image_owner, text_len, weights, top_grad):
    channels = txt_embed.shape[1]
    rows = 2 * n_dp
    chips = n_dp // 2
    steps = max(chips // 2, 1)
    share = channels // n_dp
    vmem = pl.BlockSpec(memory_space=pltpu.VMEM)
    dma = pltpu.SemaphoreType.DMA
    out = pl.pallas_call(
        functools.partial(step_kernel, n_dp, pipe),
        out_shape=jax.ShapeDtypeStruct((share, channels), F32),
        in_specs=[vmem] * 5 + [pl.BlockSpec(memory_space=pl.ANY)] + [vmem] * 2,
        out_specs=vmem,
        scratch_shapes=[
            pltpu.VMEM(txt_embed.shape, BF16),
            pltpu.VMEM((channels, channels), BF16),
            pltpu.VMEM((n_dp, 2, channels), F32),
            pltpu.VMEM((n_dp, 2, channels), F32),
            pltpu.VMEM((rows, channels), F32),
            pltpu.VMEM((rows, channels), BF16),
            pltpu.VMEM((pipe, n_dp, 128), F32),
            pltpu.VMEM((pipe, rows, channels), BF16),
            pltpu.VMEM((pipe, rows, channels), BF16),
            pltpu.VMEM((pipe, rows, channels), BF16),
            pltpu.VMEM((pipe, rows, channels), BF16),
            pltpu.VMEM((pipe, rows, channels), F32),
            pltpu.VMEM((pipe, rows, channels // 2), BF16),
            pltpu.VMEM((2, pipe, rows, channels // 2), BF16),
            pltpu.VMEM((2, pipe, rows, channels), BF16),
            pltpu.VMEM((chips, 2, share // 2, channels), F32),
            pltpu.VMEM((2, steps, 2, share // 2, channels), BF16),
            pltpu.VMEM((2, steps, 2, share // 2, channels), BF16),
            dma((EMB_CHUNKS,)),
            dma((2,)),
            dma((2, steps, 2)),
            dma((2, steps, 2)),
            dma((2, steps + 1, 2)),
            dma((2, steps + 1, 2)),
            dma((2,)),
            dma(()),
            dma((pipe,)),
            dma(()),
            dma((pipe,)),
            dma((2,)),
            dma((2,)),
            dma((2, steps, 2)),
            dma((2, steps, 2)),
        ],
        compiler_params=pltpu.CompilerParams(
            collective_id=0, has_side_effects=True, vmem_limit_bytes=48 * 1024 * 1024
        ),
        name="step",
    )(
        image_owner,
        text_len,
        lat_raw.reshape(n_dp, lat_raw.shape[-1]),
        txt_raw.reshape(n_dp, txt_raw.shape[-1]),
        lat_embed,
        txt_embed,
        weights[0],
        top_grad[0, 0],
    )
    return out[None]


def solution(mesh, pipe=8):
    placed = (
        P("section", None, "dp", None),
        P("section", None, "dp", None),
        P(),
        P(),
        P(),
        P(),
        P("section", "dp", None),
        P("dp", "section", None, None),
    )
    return jax.shard_map(
        functools.partial(local, pipe, mesh.shape["dp"]),
        mesh=mesh,
        in_specs=placed,
        out_specs=P("section", "dp", None),
        check_vma=False,
    )
```

```python
import functools

import jax
import jax.numpy as jnp
from jax import lax
from jax.experimental import pallas as pl
from jax.experimental.pallas import tpu as pltpu
from jax.sharding import PartitionSpec as P

NORM_EPS = 1e-06
MESH = pl.DeviceIdType.MESH
F32 = jnp.float32
BF16 = jnp.bfloat16
EMB_CHUNKS = 8
PARTS = 4
FWD_CHUNKS = 2


def step_kernel(
    n_dp,
    pipe,
    owner_hbm,
    len_hbm,
    lat_hbm,
    txt_hbm,
    lat_emb_hbm,
    emb_hbm,
    w_hbm,
    top_hbm,
    out_ref,
    owner_ref,
    len_ref,
    lat_ref,
    txt_ref,
    lat_emb_ref,
    emb,
    wfull,
    route_out,
    route_in,
    rows_f32,
    x0,
    coef,
    xin,
    xout,
    gin,
    gout,
    gate_slope,
    hid_send,
    hid,
    slopes,
    partial,
    rs_out,
    rs_in,
    emb_sem,
    in_sem,
    route_sem,
    w_send,
    w_recv,
    pw_send,
    pw_recv,
    feed_sem,
    x_send,
    x_recv,
    g_send,
    g_recv,
    h_sem,
    s_sem,
    r_send,
    r_recv,
):
    chips = n_dp // 2
    half_ring = chips // 2
    channels = wfull.shape[0]
    share = channels // n_dp
    half = share // PARTS
    rows = 2 * n_dp
    me = lax.axis_index("dp")
    section = lax.axis_index("section")
    pos = lax.rem(section, pipe)
    first = section - pos
    last = first + pipe - 1
    chip = lax.div(me, 2)
    core = lax.rem(me, 2)
    partner = chip * 2 + 1 - core
    beside = first + lax.rem(pos + 1, max(pipe, 1))

    def remote(src, dst, send, recv, **where):
        return pltpu.make_async_remote_copy(
            src_ref=src,
            dst_ref=dst,
            send_sem=send,
            recv_sem=recv,
            device_id=where,
            device_id_type=MESH,
        )

    depth = emb.shape[0] // EMB_CHUNKS

    def emb_copy(i):
        part = pl.ds(i * depth, depth)
        return pltpu.make_async_copy(emb_hbm.at[part], emb.at[part], emb_sem.at[i])

    own_rows = wfull.at[pl.ds(pl.multiple_of(me * share, share), share)]
    fetches = [
        pltpu.make_async_copy(src, dst, in_sem.at[i])
        for i, (src, dst) in enumerate(
            (
                (w_hbm, own_rows),
                (owner_hbm, owner_ref),
                (len_hbm, len_ref),
                (lat_hbm, lat_ref),
                (txt_hbm, txt_ref),
                (lat_emb_hbm, lat_emb_ref),
            )
        )
    ]
    for fetch in fetches:
        fetch.start()
    for i in range(EMB_CHUNKS):
        emb_copy(i).start()

    barrier = pltpu.get_barrier_semaphore()
    for k in range(1, n_dp):
        pl.semaphore_signal(
            barrier, inc=1, device_id={"dp": lax.rem(me + k, n_dp)}, device_id_type=MESH
        )
    for k in range(1, pipe):
        pl.semaphore_signal(
            barrier,
            inc=1,
            device_id={"section": first + lax.rem(pos + k, pipe)},
            device_id_type=MESH,
        )

    for fetch in fetches:
        fetch.wait()
    columns = owner_ref.shape[1]
    column = lax.broadcasted_iota(jnp.int32, (1, columns), 1)
    counts = jnp.sum(
        jnp.where(owner_ref[...] == me, len_ref[...], 0).astype(F32), axis=0, keepdims=True
    )
    order = lax.broadcasted_iota(jnp.int32, (n_dp, 128), 0).astype(F32)
    for m in range(pipe):
        count = jnp.sum(jnp.where(column == first + m, counts, 0.0), axis=1, keepdims=True)
        count = jnp.broadcast_to(count, (n_dp, 128))
        coef[m] = jnp.where(order < count, 0.5 / count, 0.0)
    owners = jnp.sum(
        jnp.where(column == section, owner_ref[...], 0).astype(F32), axis=1, keepdims=True
    )
    spot = lax.broadcasted_iota(jnp.int32, (n_dp, n_dp), 1).astype(F32)
    pick = (spot == owners).astype(F32).astype(BF16)
    pl.semaphore_wait(barrier, n_dp - 1 + pipe - 1)

    def w_block(owner_chip, whose, h):
        start = (owner_chip * 2 + whose) * share + h * half
        return wfull.at[pl.ds(pl.multiple_of(start, half), half)]

    def origin(direction, t):
        step = t if direction == 0 else chips - t
        return lax.rem(chip - step + 2 * chips, chips) if direction == 0 else lax.rem(chip + t, chips)

    def ahead(direction):
        step = 1 if direction == 0 else chips - 1
        return lax.rem(chip + step, chips) * 2 + core

    every = tuple(range(PARTS))

    def side(direction):
        return every[: PARTS // 2] if direction == 0 else every[PARTS // 2 :]

    def halves(direction, t):
        return side(direction) if t == half_ring else every

    def w_hop(direction, t, h):
        blk = w_block(origin(direction, t - 1) if t > 1 else chip, core, h)
        return remote(
            blk, blk, w_send.at[direction, t - 1, h], w_recv.at[direction, t - 1, h], dp=ahead(direction)
        )

    def w_land(direction, t, h):
        dst = w_block(origin(direction, t), core, h)
        return remote(
            dst, dst, w_send.at[direction, t - 1, h], w_recv.at[direction, t - 1, h], dp=ahead(direction)
        )

    def w_share(direction, t, h):
        blk = w_block(origin(direction, t), core, h)
        return remote(blk, blk, pw_send.at[direction, t, h], pw_recv.at[direction, t, h], dp=partner)

    def w_shared(direction, t, h):
        blk = w_block(origin(direction, t), 1 - core, h)
        return remote(blk, blk, pw_send.at[direction, t, h], pw_recv.at[direction, t, h], dp=partner)

    def w_own():
        return remote(own_rows, own_rows, pw_send.at[0, 0, 0], pw_recv.at[0, 0, 0], dp=partner)

    def w_owned():
        blk = wfull.at[pl.ds(pl.multiple_of(partner * share, share), share)]
        return remote(blk, blk, pw_send.at[0, 0, 0], pw_recv.at[0, 0, 0], dp=partner)

    if half_ring:
        for h in range(PARTS):
            for direction in (0, 1):
                if h in halves(direction, 1):
                    w_hop(direction, 1, h).start()
    w_own().start()

    def top_feed(slot):
        return remote(top_hbm, gin.at[slot], feed_sem.at[0], g_recv.at[slot], section=last)

    @pl.when(pos < pipe - 1)
    def _():
        top_feed(pipe - 1 - pos).start()

    @pl.when(pos == pipe - 1)
    def _():
        pltpu.make_async_copy(top_hbm, gin.at[0], g_recv.at[0]).start()

    def encode(i, so_far):
        emb_copy(i).wait()
        part = pl.ds(i * depth, depth)
        return so_far + jnp.dot(txt_ref[:, part], emb[part, :], preferred_element_type=F32)

    def ring_step(t):
        for h in range(PARTS):
            for direction in (0, 1):
                if h in halves(direction, t):
                    w_land(direction, t, h).wait_recv()
                    if t < half_ring and h in halves(direction, t + 1):
                        w_hop(direction, t + 1, h).start()
                    w_share(direction, t, h).start()

    text = jnp.zeros((n_dp, channels), F32)
    for i in range(EMB_CHUNKS):
        text = encode(i, text)
    lat = jnp.dot(lat_ref[...], lat_emb_ref[...], preferred_element_type=F32)
    over_rows = (((0,), (0,)), ((), ()))
    lat_sel = lax.dot_general(pick, lat.astype(BF16), over_rows, preferred_element_type=F32)
    text_sel = lax.dot_general(pick, text.astype(BF16), over_rows, preferred_element_type=F32)
    for i in range(n_dp):
        route_out[i, 0:1, :] = lat_sel[i : i + 1, :]
        route_out[i, 1:2, :] = text_sel[i : i + 1, :]

    def route(k):
        to = lax.rem(me + k, n_dp)
        return remote(route_out.at[to], route_in.at[me], route_sem.at[0], route_sem.at[1], dp=to)

    for k in range(1, n_dp):
        route(k).start()
    route_in[me] = route_out[me]
    if half_ring:
        ring_step(1)

    several = pl.ds(0, n_dp - 1)
    routed = remote(
        route_out.at[several], route_in.at[several], route_sem.at[0], route_sem.at[1], dp=partner
    )
    routed.wait_recv()
    for i in range(n_dp):
        rows_f32[i : i + 1, :] = route_in[i, 0:1, :]
        rows_f32[n_dp + i : n_dp + i + 1, :] = route_in[i, 1:2, :]
    x0[...] = rows_f32[...].astype(BF16)

    def row_feed(slot):
        return remote(x0, xin.at[slot], feed_sem.at[1], x_recv.at[slot], section=first)

    @pl.when(pos > 0)
    def _():
        row_feed(pos).start()

    @pl.when(pos == 0)
    def _():
        xin[0] = rows_f32[...].astype(BF16)

    for t in range(2, half_ring + 1):
        ring_step(t)
    w_owned().wait_recv()
    for t in range(1, half_ring + 1):
        for h in range(PARTS):
            for direction in (0, 1):
                if h in halves(direction, t):
                    w_shared(direction, t, h).wait_recv()

    text_rows = slice(n_dp, rows)
    low = lax.broadcasted_iota(jnp.int32, (rows, 128), 1) < 64
    spread = channels // 128

    def wide(column):
        return jnp.concatenate([column] * spread, axis=1)

    def normed(m):
        x = xin[m].astype(F32)
        inv = lax.rsqrt(jnp.mean(x * x, axis=1, keepdims=True) + NORM_EPS)
        u = x * inv
        pooled = jnp.sum(u[text_rows, :] * wide(coef[m]), axis=0, keepdims=True)
        return x, inv, u, 1.0 + pooled

    cols = channels // FWD_CHUNKS

    def x_hop(m, n):
        part = pl.ds(n * cols, cols)
        return remote(
            xout.at[m, :, part], xin.at[m, :, part], x_send, x_recv.at[m], section=section + 1
        )

    def hid_hop(m):
        return remote(hid_send.at[m], hid.at[1, m], h_sem.at[0], h_sem.at[1], dp=partner)

    def slope_hop(m):
        return remote(slopes.at[0, m], slopes.at[1, m], s_sem.at[0], s_sem.at[1], dp=partner)

    def forward(m):
        @pl.when((pos > 0) | (m > 0))
        def _():
            remote(xout.at[m], xin.at[m], x_send, x_recv.at[m], section=beside).wait_recv()

        x, inv, u, scale = normed(m)
        hidden_wide = u * scale
        hidden = hidden_wide.astype(BF16)
        for n in range(FWD_CHUNKS):
            part = slice(n * cols, (n + 1) * cols)
            pre = jnp.dot(hidden, wfull[:, part], preferred_element_type=F32)
            sig = jax.nn.sigmoid(pre)
            xout[m, :, part] = (x[:, part] + pre * sig).astype(BF16)

            @pl.when(pos < pipe - 1)
            def _():
                x_hop(m, n).start()

            gate_slope[m, :, part] = sig * (1.0 + pre * (1.0 - sig))
        for k in range(chips // 2):
            a = hidden_wide[:, 256 * k : 256 * k + 128]
            b = hidden_wide[:, 256 * k + 128 : 256 * k + 256]
            lo = jnp.where(low, a, pltpu.roll(b, 64, 1))
            hi = jnp.where(low, pltpu.roll(a, 64, 1), b)
            place = slice(128 * k, 128 * k + 128)
            is_low = core == 0
            hid[0, m, :, place] = jnp.where(is_low, lo, hi).astype(BF16)
            hid_send[m, :, place] = jnp.where(is_low, hi, lo).astype(BF16)
        hid_hop(m).start()

    def g_hop(m):
        return remote(gout.at[m], gin.at[m], g_send, g_recv.at[m], section=section - 1)

    def backward(m):
        x, inv, u, scale = normed(m)

        remote(gout.at[m], gin.at[m], g_send, g_recv.at[m], section=beside).wait_recv()
        g = gin[m].astype(F32)
        slope = (g * gate_slope[m]).astype(BF16)
        slopes[0, m] = slope
        slope_hop(m).start()

        @pl.when(pos > 0)
        def _():
            back = lax.dot_general(
                slope, wfull[...], (((1,), (1,)), ((), ())), preferred_element_type=F32
            )
            to_pool = jnp.sum(back * u, axis=0, keepdims=True)
            gu = back * scale
            gu = jnp.concatenate(
                [gu[:n_dp, :], gu[text_rows, :] + wide(coef[m]) * to_pool], axis=0
            )
            along = jnp.mean(gu * u, axis=1, keepdims=True)
            gout[m] = (g + inv * (gu - u * along)).astype(BF16)
            g_hop(m).start()

    lag = jnp.where(pos == pipe - 1, 0, jnp.where(pos == pipe - 2, max(pipe - 2, 0), pipe - 1))

    def turn(t, carry):
        @pl.when(t < pipe)
        def _():
            forward(t)

        @pl.when((t >= lag) & (t < lag + pipe))
        def _():
            backward(t - lag)

        return carry

    lax.fori_loop(0, 2 * pipe - 1, turn, 0)

    def all_hid():
        return remote(hid_send, hid.at[1], h_sem.at[0], h_sem.at[1], dp=partner)

    def all_slopes():
        return remote(slopes.at[0], slopes.at[1], s_sem.at[0], s_sem.at[1], dp=partner)

    all_hid().wait_recv()
    all_slopes().wait_recv()
    deep = 2 * pipe * rows
    cotangents = slopes[...].reshape(deep, channels)
    for k in range(chips // 2):
        held = hid[:, :, :, 128 * k : 128 * k + 128].reshape(deep, 128)
        both = lax.dot_general(
            held, cotangents, (((0,), (0,)), ((), ())), preferred_element_type=F32
        )
        for j in (0, 1):
            for h in range(PARTS):
                at = 64 * j + half * h
                partial[2 * k + j, h] = both[at : at + half, :]

    def r_hop(direction, t, h):
        return remote(
            rs_out.at[direction, t - 1, h],
            rs_in.at[direction, t - 1, h],
            r_send.at[direction, t - 1, h],
            r_recv.at[direction, t - 1, h],
            dp=ahead(direction),
        )

    def r_halves(direction, t):
        return side(direction) if t == 1 else every

    for t in range(1, half_ring + 1):
        gap = half_ring - t + 1
        for h in range(PARTS):
            for direction in (0, 1):
                if h in r_halves(direction, t):
                    to = lax.rem(chip + (gap if direction == 0 else chips - gap), chips)
                    total = partial[to, h]
                    if t > 1 and h in r_halves(direction, t - 1):
                        r_hop(direction, t - 1, h).wait_recv()
                        total = total + rs_in[direction, t - 2, h].astype(F32)
                    rs_out[direction, t - 1, h] = total.astype(BF16)
                    r_hop(direction, t, h).start()
    for h in range(PARTS):
        total = partial[chip, h]
        for direction in (0, 1):
            if half_ring and h in r_halves(direction, half_ring):
                r_hop(direction, half_ring, h).wait_recv()
                total = total + rs_in[direction, half_ring - 1, h].astype(F32)
        out_ref[h * half : (h + 1) * half, :] = total

    for t in range(1, half_ring + 1):
        for h in range(PARTS):
            for direction in (0, 1):
                if h in halves(direction, t):
                    w_hop(direction, t, h).wait_send()
                    w_share(direction, t, h).wait_send()
                if h in r_halves(direction, t):
                    r_hop(direction, t, h).wait_send()
    w_own().wait_send()
    routed.wait_send()
    all_hid().wait_send()
    all_slopes().wait_send()

    @pl.when(pos < pipe - 1)
    def _():
        top_feed(1).wait_send()
        remote(xout, xin, x_send, x_recv.at[0], section=beside).wait_send()

    @pl.when(pos > 0)
    def _():
        row_feed(0).wait_send()
        remote(gout, gin, g_send, g_recv.at[0], section=beside).wait_send()


def local(pipe, n_dp, lat_raw, txt_raw, lat_embed, txt_embed, image_owner, text_len, weights, top_grad):
    channels = txt_embed.shape[1]
    rows = 2 * n_dp
    chips = n_dp // 2
    steps = max(chips // 2, 1)
    share = channels // n_dp
    vmem = pl.BlockSpec(memory_space=pltpu.VMEM)
    dma = pltpu.SemaphoreType.DMA
    out = pl.pallas_call(
        functools.partial(step_kernel, n_dp, pipe),
        out_shape=jax.ShapeDtypeStruct((share, channels), F32),
        in_specs=[pl.BlockSpec(memory_space=pl.ANY)] * 8,
        out_specs=vmem,
        scratch_shapes=[
            pltpu.VMEM(image_owner.shape[::-1], jnp.int32),
            pltpu.VMEM(image_owner.shape[::-1], jnp.int32),
            pltpu.VMEM((n_dp, lat_raw.shape[-1]), BF16),
            pltpu.VMEM((n_dp, txt_raw.shape[-1]), BF16),
            pltpu.VMEM(lat_embed.shape, BF16),
            pltpu.VMEM(txt_embed.shape, BF16),
            pltpu.VMEM((channels, channels), BF16),
            pltpu.VMEM((n_dp, 2, channels), F32),
            pltpu.VMEM((n_dp, 2, channels), F32),
            pltpu.VMEM((rows, channels), F32),
            pltpu.VMEM((rows, channels), BF16),
            pltpu.VMEM((pipe, n_dp, 128), F32),
            pltpu.VMEM((pipe, rows, channels), BF16),
            pltpu.VMEM((pipe, rows, channels), BF16),
            pltpu.VMEM((pipe, rows, channels), BF16),
            pltpu.VMEM((pipe, rows, channels), BF16),
            pltpu.VMEM((pipe, rows, channels), F32),
            pltpu.VMEM((pipe, rows, channels // 2), BF16),
            pltpu.VMEM((2, pipe, rows, channels // 2), BF16),
            pltpu.VMEM((2, pipe, rows, channels), BF16),
            pltpu.VMEM((chips, PARTS, share // PARTS, channels), F32),
            pltpu.VMEM((2, steps, PARTS, share // PARTS, channels), BF16),
            pltpu.VMEM((2, steps, PARTS, share // PARTS, channels), BF16),
            dma((EMB_CHUNKS,)),
            dma((6,)),
            dma((2,)),
            dma((2, steps, PARTS)),
            dma((2, steps, PARTS)),
            dma((2, steps + 1, PARTS)),
            dma((2, steps + 1, PARTS)),
            dma((2,)),
            dma(()),
            dma((pipe,)),
            dma(()),
            dma((pipe,)),
            dma((2,)),
            dma((2,)),
            dma((2, steps, PARTS)),
            dma((2, steps, PARTS)),
        ],
        compiler_params=pltpu.CompilerParams(
            collective_id=0, has_side_effects=True, vmem_limit_bytes=60 * 1024 * 1024
        ),
        name="step",
    )(
        image_owner.T,
        text_len.T,
        lat_raw.reshape(n_dp, lat_raw.shape[-1]),
        txt_raw.reshape(n_dp, txt_raw.shape[-1]),
        lat_embed,
        txt_embed,
        weights[0],
        top_grad[0, 0],
    )
    return out[None]


def solution(mesh, pipe=8):
    placed = (
        P("section", None, "dp", None),
        P("section", None, "dp", None),
        P(),
        P(),
        P(),
        P(),
        P("section", "dp", None),
        P("dp", "section", None, None),
    )
    return jax.shard_map(
        functools.partial(local, pipe, mesh.shape["dp"]),
        mesh=mesh,
        in_specs=placed,
        out_specs=P("section", "dp", None),
        check_vma=False,
    )
```
